32 devices in a mesh: ulysses: 4 (over z), blk: 2 (over y), tensor: 4 (over x, core).
Axes of the slice: x: 2, y: 2, z: 4, core: 2. Of those that a mesh axis runs over, the one named last changes fastest.
Arguments:
- tokens: bfloat16 [2048, 5120], P(('ulysses', 'blk'), 'tensor'), may hold values from -20 to 20
- w_qkv: bfloat16 [5120, 3, 4096], P(None, None, ('ulysses', 'tensor')), may hold values from -2 to 2
- qkv_scale: float32 [3, 32], P(None, ('ulysses', 'tensor')), may hold values from 0.6 to 9
- block_mask: int32 [32, 16, 16], P(('ulysses', 'tensor')), may hold values from 0 to 1, as said below
- w_out: bfloat16 [4, 1024, 5120], P(None, 'tensor'), may hold values from -0.125 to 0.125
Outputs:
- mixed: bfloat16 [2048, 5120], P(('ulysses', 'blk'), 'tensor')
The draws below stay inside these ranges and needn't reach their ends.
Inputs may be any that keep to these rules, and one draw needn't show every extreme that they name: `block_mask`: 0 or 1; the share of ones differs from head to head.
All inputs are finite; a program needn't handle non-finite values.
Results may differ from the reference program's by a relative error of at most 0.015.
Values may be sent and summed in bfloat16 or wider, within the bound.
A program may use at most 128 MiB of HBM per device.

```python
import math
import jax
import jax.numpy as jnp
from jax import lax

D = 5120
HD = 128
HPD = 2
BLOCK = 128
HEADS = 32
TOKENS = 2048
NB = 16
N_ULYSSES = 4
N_TENSOR = 4


def draw_block_mask(key, part):
    dense_key = jax.random.fold_in(key, 11)
    cell_key = jax.random.fold_in(key, 12)
    density = jax.random.randint(dense_key, (HEADS, 1, 1), 1, 8)
    cells = jax.random.randint(cell_key, (HEADS, NB, NB), 0, 8)
    return (cells < density).astype(jnp.int32)


def head_law(key):
    order_key = jax.random.fold_in(key, 21)
    base_key = jax.random.fold_in(key, 22)
    strong_key = jax.random.fold_in(key, 23)
    temper_key = jax.random.fold_in(key, 24)
    coupling_key = jax.random.fold_in(key, 25)
    ranking = jax.random.permutation(order_key, HEADS)
    strong = ranking < HEADS // 4
    base = jnp.exp(jax.random.uniform(base_key, (3, HEADS), jnp.float32, jnp.log(0.6), jnp.log(2.0)))
    high = jnp.exp(jax.random.uniform(strong_key, (3, HEADS), jnp.float32, jnp.log(5.0), jnp.log(9.0)))
    query_key_rows = (jnp.arange(3, dtype=jnp.int32) < 2)[:, None]
    chosen = jnp.where(query_key_rows & strong[None, :], high, base).astype(jnp.float32)
    temper = jnp.exp(jax.random.uniform(temper_key, (HEADS,), jnp.float32, jnp.log(0.8), jnp.log(2.0)))
    coupling = jax.random.uniform(coupling_key, (HEADS,), jnp.float32, 0.75, 1.0)
    return (chosen, temper, coupling)


def draw_qkv_scale(key, part):
    chosen, temper, coupling = head_law(key)
    return chosen


def draw_w_qkv(key, part):
    chosen, temper, coupling = head_law(key)
    column_gain = jnp.sqrt(temper / (chosen[0] * chosen[1]))
    query_key = jax.random.fold_in(key, 31)
    other_key = jax.random.fold_in(key, 32)
    value_key = jax.random.fold_in(key, 33)
    shape = (D, HEADS * HD)
    query_noise = jax.random.truncated_normal(query_key, -4.0, 4.0, shape, jnp.float32)
    other_noise = jax.random.truncated_normal(other_key, -4.0, 4.0, shape, jnp.float32)
    value_noise = jax.random.truncated_normal(value_key, -4.0, 4.0, shape, jnp.float32)
    head_gain = jnp.repeat(column_gain, HD)[None, :]
    head_coupling = jnp.repeat(coupling, HD)[None, :]
    spread = 1.0 / jnp.sqrt(jnp.float32(D))
    query_cols = head_gain * query_noise * spread
    key_cols = head_gain * (head_coupling * query_noise + jnp.sqrt(1.0 - head_coupling * head_coupling) * other_noise) * spread
    value_cols = value_noise * spread
    return jnp.stack([query_cols, key_cols, value_cols], axis=1).astype(jnp.bfloat16)


def draw_tokens(key, part):
    noise_key = jax.random.fold_in(key, 41)
    direction_key = jax.random.fold_in(key, 42)
    member_key = jax.random.fold_in(key, 43)
    polarity_key = jax.random.fold_in(key, 44)
    strength_key = jax.random.fold_in(key, 45)
    noise = jax.random.truncated_normal(noise_key, -4.0, 4.0, (TOKENS, D), jnp.float32)
    largest = 2.5
    directions = jax.random.truncated_normal(direction_key, -4.0, 4.0, (16, D), jnp.float32)
    member = jax.random.randint(member_key, (TOKENS,), 0, 16)
    polarity = jnp.where(jax.random.randint(polarity_key, (TOKENS,), 0, 2) == 1, 1.0, -1.0)
    strength = jax.random.uniform(strength_key, (TOKENS,), jnp.float32, 0.0, largest)
    shared = jnp.take(directions, member, axis=0)
    return (noise + (polarity * strength)[:, None] * shared).astype(jnp.bfloat16)


def block_scale(stream_key, dims, pieces, low, high):
    loudness, own = 1.0, jax.random.fold_in(stream_key, 6)
    for dim, blocks in pieces:
        heights = jnp.exp(jax.random.uniform(jax.random.fold_in(own, dim), (blocks,), jnp.float32, low / len(pieces), high / len(pieces)))
        loudness = loudness * jnp.repeat(heights, dims[dim] // blocks).reshape([-1 if axis == dim else 1 for axis in range(len(dims))])
    return loudness


def gaussian(stream_key, extent, scale, most, split=(), held_as=jnp.bfloat16):
    result = scale * jax.random.normal(stream_key, extent, jnp.float32)
    if split:
        result = result * block_scale(stream_key, extent, split, -0.22, 0.18)
    return jnp.clip(result, -most, most).astype(held_as)


def setup_inputs(seed: int = 0) -> dict:
    seeds = jax.random.split(jax.random.key(seed), 6)
    return {
        "tokens": draw_tokens(jax.random.fold_in(seeds[5], 71), 0),
        "w_qkv": draw_w_qkv(jax.random.fold_in(seeds[5], 71), 0),
        "qkv_scale": draw_qkv_scale(jax.random.fold_in(seeds[5], 71), 0),
        "block_mask": draw_block_mask(jax.random.fold_in(seeds[5], 71), 0),
        "w_out": gaussian(seeds[4], (N_ULYSSES, N_TENSOR * HPD * HD, D), (HPD * HD * 8) ** -0.5, 0.125, ((1, 4),)),
    }


def attend_head(queries, keys, values, head_mask):
    key_blocks = jnp.arange(TOKENS, dtype=jnp.int32) // BLOCK
    score_scale = 1.0 / math.sqrt(HD)

    def one_block(position):
        query_rows = lax.dynamic_slice_in_dim(queries, (position * BLOCK).astype(jnp.int32), BLOCK, 0)
        scores = jnp.dot(query_rows, keys.T, preferred_element_type=jnp.float32) * score_scale
        allowed = (head_mask[position][key_blocks] == 1) | (key_blocks == position)
        scores = jnp.where(allowed[None, :], scores, -jnp.inf)
        highest = lax.optimization_barrier(jnp.max(scores, axis=-1, keepdims=True))
        weights = jnp.exp(scores - highest)
        denominator = lax.optimization_barrier(jnp.sum(weights, axis=-1, keepdims=True))
        summed = jnp.dot(weights.astype(jnp.bfloat16), values, preferred_element_type=jnp.float32)
        return summed / denominator
    return lax.map(one_block, jnp.arange(NB, dtype=jnp.int32))

def reference(tokens, w_qkv, qkv_scale, block_mask, w_out):
    matrix = w_qkv.reshape(D, 3 * HEADS * HD)
    projected = jnp.dot(tokens, matrix, preferred_element_type=jnp.float32).reshape(TOKENS, 3, HEADS, HD)
    projected = (projected * qkv_scale[None, :, :, None]).astype(jnp.bfloat16)

    def per_head(head_index):
        return attend_head(projected[:, 0, head_index], projected[:, 1, head_index], projected[:, 2, head_index], block_mask[head_index])
    attended = lax.map(per_head, jnp.arange(HEADS, dtype=jnp.int32))
    attended = attended.astype(jnp.bfloat16).reshape(HEADS, TOKENS, HD)
    attended = jnp.transpose(attended, (1, 0, 2)).reshape(TOKENS, HEADS * HD)
    mixed = jnp.dot(attended, w_out.reshape(HEADS * HD, D), preferred_element_type=jnp.float32)
    return mixed.astype(jnp.bfloat16)
```

```python
import functools
import math

import jax
import jax.numpy as jnp
from jax import lax
from jax.experimental import pallas as pl
from jax.experimental.pallas import tpu as pltpu
from jax.sharding import PartitionSpec as P

SUB = 2
F32 = jnp.float32
BF16 = jnp.bfloat16


def kernel(U, B, T, x_ref, w_hbm, scale_ref, bias_ref, wo_hbm, out_ref,
           g, w, wo, q, kv, att, arr, part, got, mid, far_got,
           w_sem, wo_sem, own_sem,
           zs, zr, up_s, dn_s, xs, xr, cs, cr, fs, fr, ks, kr, as_, ar, ps, pr, ms, mr):
    z, y, t = lax.axis_index("ulysses"), lax.axis_index("blk"), lax.axis_index("tensor")
    near = t + 1 - 2 * lax.rem(t, 2)
    far = lax.rem(t + T // 2, T)
    cross = lax.rem(near + T // 2, T)
    rows, feats = x_ref.shape
    R = rows // SUB
    H, HD = q.shape[0], q.shape[2]
    N = U * SUB
    nbp = rows // bias_ref.shape[3]
    block = bias_ref.shape[3]

    w_copy = pltpu.make_async_copy(w_hbm, w, w_sem)
    w_copy.start()
    wo_copies = [
        pltpu.make_async_copy(wo_hbm.at[:, :, pl.ds(j * feats, feats)], wo.at[j], wo_sem.at[j])
        for j in range(T)
    ]
    for c in wo_copies:
        c.start()
    for s in range(SUB):
        c = pltpu.make_async_copy(x_ref.at[pl.ds(s * R, R)], g.at[z * SUB + s, t], own_sem.at[s])
        c.start()
    for s in range(SUB):
        pltpu.make_async_copy(x_ref.at[pl.ds(s * R, R)], g.at[z * SUB + s, t], own_sem.at[s]).wait()

    barrier = pltpu.get_barrier_semaphore()
    for d in range(1, U):
        pl.semaphore_signal(barrier, inc=1, device_id={"ulysses": lax.rem(z + d, U)})
    for d in range(1, B):
        pl.semaphore_signal(barrier, inc=1, device_id={"blk": lax.rem(y + d, B)})
    pl.semaphore_signal(barrier, inc=1, device_id={"tensor": near})
    pl.semaphore_signal(barrier, inc=1, device_id={"tensor": far})
    pl.semaphore_wait(barrier, (U - 1) + (B - 1) + 2)

    def order(p):
        m = jnp.minimum(z, U - 1 - z)
        half = (p + 1) // 2
        near_z = jnp.where(lax.rem(p, 2) == 1, z - half, z + half)
        far_z = jnp.where(z < U - 1 - z, p, U - 1 - p)
        return jnp.where(p <= 2 * m, near_z, far_z)

    def remote(src, dst, send, recv, **where):
        return pltpu.make_async_remote_copy(
            src_ref=src, dst_ref=dst, send_sem=send, recv_sem=recv, device_id=where
        )

    def piece_of(i):
        zz = order(i // SUB)
        return zz, zz * SUB + lax.rem(i, SUB)

    def z_copy(slot, send, target):
        return remote(g.at[slot, t], g.at[slot, t], send, zr.at[slot], ulysses=target)

    def x_copy(slot, col, i):
        return remote(g.at[slot, col], g.at[slot, col], xs.at[i], xr.at[i], tensor=far)

    def c_copy(slot, col, i):
        return remote(g.at[slot, col], g.at[slot, col], cs.at[i], cr.at[i], tensor=near)

    def f_copy(slot, col, i):
        return remote(g.at[slot, col], g.at[slot, col], fs.at[i], fr.at[i], tensor=near)

    def kv_copy(who, slot, i, d):
        view = kv.at[who, :, :, pl.ds(pl.multiple_of(slot * R, R), R), :]
        return remote(view, view, ks.at[d - 1, i], kr.at[who, i], blk=lax.rem(y + d, B))

    def forward(i, act):
        zz, slot = piece_of(i)
        own = i < SUB
        s = lax.rem(i, SUB)

        @pl.when(own & (z + 1 < U))
        def _():
            act(z_copy(slot, up_s.at[s], z + 1))

        @pl.when(own & (z > 0))
        def _():
            act(z_copy(slot, dn_s.at[s], z - 1))

        nxt = jnp.where(zz < z, z + 1, z - 1)

        @pl.when(jnp.logical_not(own) & (nxt >= 0) & (nxt < U))
        def _():
            act(z_copy(slot, zs.at[slot], nxt))

    def step(j, carry):
        @pl.when(j < N)
        def _():
            zz, slot = piece_of(j)

            @pl.when(j >= SUB)
            def _():
                z_copy(slot, zs.at[slot], lax.rem(z + 1, U)).wait_recv()

            forward(j, lambda c: c.start())
            x_copy(slot, t, j).start()
            c_copy(slot, t, j).start()

        @pl.when(j >= SUB)
        def _():
            i = j - SUB
            zz, slot = piece_of(i)
            x_copy(slot, far, i).wait_recv()
            f_copy(slot, far, i).start()
            c_copy(slot, near, i).wait_recv()

            @pl.when(i == 0)
            def _():
                w_copy.wait()

            f_copy(slot, cross, i).wait_recv()
            for c in range(3):
                acc = jnp.zeros((R, H * HD), F32)
                for k in range(T):
                    acc += jnp.dot(
                        g[slot, k], w[c, pl.ds(k * feats, feats), :], preferred_element_type=F32
                    )
                for h in range(H):
                    val = (acc[:, h * HD:(h + 1) * HD] * scale_ref[c, h]).astype(BF16)
                    at = pl.ds(pl.multiple_of(slot * R, R), R)
                    if c == 0:
                        q[h, at, :] = val
                    else:
                        kv[y, c - 1, h, at, :] = val
            for d in range(1, B):
                kv_copy(y, slot, i, d).start()

        return carry

    lax.fori_loop(0, N + SUB, step, 0)

    def kv_wait(i, carry):
        zz, slot = piece_of(i)
        for d in range(1, B):
            kv_copy(lax.rem(y + d, B), slot, i, d).wait_recv()
        return carry

    lax.fori_loop(0, N, kv_wait, 0)

    log2e = 1.4426950408889634
    factor = log2e / math.sqrt(HD)

    def a_copy(zz, src):
        return remote(att.at[zz], arr.at[src], as_.at[zz], ar.at[src], ulysses=zz)

    def attend(p, carry):
        zz = order(U - 1 - p)
        for h in range(H):
            qv = q[h, pl.ds(pl.multiple_of(zz * rows, rows), rows), :]

            def keys(b, state):
                high, den, num = state
                s = lax.dot_general(
                    qv, kv[b, 0, h], (((1,), (1,)), ((), ())), preferred_element_type=F32
                )
                lines = []
                for r in range(nbp):
                    qb = (zz * B + y) * nbp + r
                    lines.append(
                        jnp.concatenate(
                            [
                                bias_ref[h, qb, pl.ds((k // nbp * B + b) * nbp + k % nbp, 1), :]
                                for k in range(U * nbp)
                            ],
                            axis=1,
                        )
                    )
                s = jnp.concatenate(
                    [s[r * block:(r + 1) * block] * factor + lines[r] for r in range(nbp)], axis=0
                )
                new = jnp.maximum(high, jnp.max(s, axis=1, keepdims=True))
                wts = jnp.exp2(s - new)
                fix = jnp.exp2(high - new)
                den = den * fix + jnp.sum(wts, axis=1, keepdims=True)
                num = num * fix + jnp.dot(
                    wts.astype(BF16), kv[b, 1, h], preferred_element_type=F32
                )
                return new, den, num

            start = (
                jnp.full((rows, 1), -1e30, F32),
                jnp.zeros((rows, 1), F32),
                jnp.zeros((rows, HD), F32),
            )
            high, den, num = lax.fori_loop(0, B, keys, start)
            att[zz, :, h * HD:(h + 1) * HD] = (num / den).astype(BF16)

        @pl.when(p < U - 1)
        def _():
            a_copy(zz, z).start()

        return carry

    lax.fori_loop(0, U, attend, 0)
    arr[z] = att[z]
    for c in wo_copies:
        c.wait()
    for d in range(1, U):
        a_copy(lax.rem(z + d, U), lax.rem(z + d, U)).wait_recv()

    def product(col):
        acc = jnp.dot(arr[0], wo[col, 0], preferred_element_type=F32)
        for u in range(1, U):
            acc += jnp.dot(arr[u], wo[col, u], preferred_element_type=F32)
        return acc

    def p_copy(k):
        return remote(part.at[k], got.at[k], ps.at[k], pr.at[k], tensor=near)

    m_copy = remote(mid, far_got, ms, mr, tensor=far)
    part[0] = product(cross).astype(BF16)
    p_copy(0).start()
    there = product(far)
    p_copy(0).wait_recv()
    mid[...] = (there + got[0].astype(F32)).astype(BF16)
    m_copy.start()
    part[1] = product(near).astype(BF16)
    p_copy(1).start()
    here = product(t)
    p_copy(1).wait_recv()
    here = here + got[1].astype(F32)
    m_copy.wait_recv()
    out_ref[...] = (here + far_got[...].astype(F32)).astype(BF16)

    def drain(i, carry):
        zz, slot = piece_of(i)
        forward(i, lambda c: c.wait_send())
        x_copy(slot, t, i).wait_send()
        c_copy(slot, t, i).wait_send()
        f_copy(slot, far, i).wait_send()
        for d in range(1, B):
            kv_copy(y, slot, i, d).wait_send()
        return carry

    lax.fori_loop(0, N, drain, 0)
    for d in range(1, U):
        a_copy(lax.rem(z + d, U), z).wait_send()
    p_copy(0).wait_send()
    p_copy(1).wait_send()
    m_copy.wait_send()


def local(tokens, w_qkv, qkv_scale, block_mask, w_out):
    U, B, T = lax.axis_size("ulysses"), lax.axis_size("blk"), lax.axis_size("tensor")
    rows, feats = tokens.shape
    heads, blocks = block_mask.shape[0], block_mask.shape[1]
    cols = w_qkv.shape[2]
    hd = cols // heads
    block = U * B * rows // blocks
    ids = jnp.arange(blocks)
    allowed = (block_mask == 1) | (ids[:, None] == ids[None, :])[None]
    bias = jnp.broadcast_to(
        jnp.where(allowed, 0.0, -jnp.inf).astype(F32)[..., None], (heads, blocks, blocks, block)
    )
    R, N = rows // SUB, U * SUB
    dma = lambda *s: pltpu.SemaphoreType.DMA(s)
    vmem = pl.BlockSpec(memory_space=pltpu.VMEM)
    hbm = pl.BlockSpec(memory_space=pl.ANY)
    return pl.pallas_call(
        functools.partial(kernel, U, B, T),
        out_shape=jax.ShapeDtypeStruct((rows, feats), BF16),
        in_specs=[vmem, hbm, pl.BlockSpec(memory_space=pltpu.SMEM), vmem, hbm],
        out_specs=vmem,
        scratch_shapes=[
            pltpu.VMEM((N, T, R, feats), BF16),
            pltpu.VMEM((3, T * feats, cols), BF16),
            pltpu.VMEM((T, U, cols, feats), BF16),
            pltpu.VMEM((heads, U * rows, hd), BF16),
            pltpu.VMEM((B, 2, heads, U * rows, hd), BF16),
            pltpu.VMEM((U, rows, cols), BF16),
            pltpu.VMEM((U, rows, cols), BF16),
            pltpu.VMEM((2, rows, feats), BF16),
            pltpu.VMEM((2, rows, feats), BF16),
            pltpu.VMEM((rows, feats), BF16),
            pltpu.VMEM((rows, feats), BF16),
            pltpu.SemaphoreType.DMA,
            dma(T),
            dma(SUB),
            dma(N), dma(N), dma(SUB), dma(SUB),
            dma(N), dma(N), dma(N), dma(N), dma(N), dma(N),
            dma(B, N), dma(B, N),
            dma(U), dma(U),
            dma(2), dma(2),
            pltpu.SemaphoreType.DMA, pltpu.SemaphoreType.DMA,
        ],
        compiler_params=pltpu.CompilerParams(
            collective_id=0, has_side_effects=True, vmem_limit_bytes=62 * 1024 * 1024
        ),
    )(tokens, jnp.transpose(w_qkv, (1, 0, 2)), qkv_scale, bias, w_out)


def solution(mesh):
    return jax.shard_map(
        local,
        mesh=mesh,
        in_specs=(
            P(("ulysses", "blk"), "tensor"),
            P(None, None, ("ulysses", "tensor")),
            P(None, ("ulysses", "tensor")),
            P(("ulysses", "tensor"), None, None),
            P(None, "tensor", None),
        ),
        out_specs=P(("ulysses", "blk"), "tensor"),
        check_vma=False,
    )
```

```python
import functools
import math

import jax
import jax.numpy as jnp
from jax import lax
from jax.experimental import pallas as pl
from jax.experimental.pallas import tpu as pltpu
from jax.sharding import PartitionSpec as P

SUB = 2
LAG = SUB + 1
F32 = jnp.float32
BF16 = jnp.bfloat16


def kernel(U, B, T, x_ref, w_hbm, scale_ref, bias_ref, wo_hbm, out_ref,
           g, w, wo, q, kv, att, arr, part, got, mid, far_got,
           w_sem, wo_sem, own_sem,
           zs, zr, up_s, dn_s, xs, xr, cs, cr, fs, fr, ks, kr, as_, ar, ps, pr, ms, mr, hs, hr):
    z, y, t = lax.axis_index("ulysses"), lax.axis_index("blk"), lax.axis_index("tensor")
    near = t + 1 - 2 * lax.rem(t, 2)
    far = lax.rem(t + T // 2, T)
    cross = lax.rem(near + T // 2, T)
    rows, feats = x_ref.shape
    R = rows // SUB
    H, HD = q.shape[0], q.shape[2]
    N = U * SUB
    nbp = rows // bias_ref.shape[3]
    block = bias_ref.shape[3]

    w_copy = pltpu.make_async_copy(w_hbm, w, w_sem)
    w_copy.start()
    wo_copies = [
        pltpu.make_async_copy(wo_hbm.at[:, :, pl.ds(j * feats, feats)], wo.at[j], wo_sem.at[j])
        for j in range(T)
    ]
    for c in wo_copies:
        c.start()
    for s in range(SUB):
        c = pltpu.make_async_copy(x_ref.at[pl.ds(s * R, R)], g.at[z * SUB + s, t], own_sem.at[s])
        c.start()
    for s in range(SUB):
        pltpu.make_async_copy(x_ref.at[pl.ds(s * R, R)], g.at[z * SUB + s, t], own_sem.at[s]).wait()

    barrier = pltpu.get_barrier_semaphore()
    for d in range(1, U):
        pl.semaphore_signal(barrier, inc=1, device_id={"ulysses": lax.rem(z + d, U)})
    for d in range(1, B):
        pl.semaphore_signal(barrier, inc=1, device_id={"blk": lax.rem(y + d, B)})
    pl.semaphore_signal(barrier, inc=1, device_id={"tensor": near})
    pl.semaphore_signal(barrier, inc=1, device_id={"tensor": far})
    pl.semaphore_wait(barrier, (U - 1) + (B - 1) + 2)

    side = 1 - 2 * lax.rem(z, 2)
    pair = z + side
    skip_from = SUB + SUB // 2
    skips = 2 * SUB - skip_from

    def skipped(j):
        return (j >= skip_from) & (j < skip_from + skips)

    def landing(i):
        late = jnp.where(i < N - skips, i + skips, i - (N - skips) + skip_from)
        return jnp.where(i < skip_from, i, late)

    def pair_copy(owner, j):
        slot = owner * SUB + SUB // 2 + j
        view = g.at[slot, far]
        return remote(view, view, hs.at[j], hr.at[j], ulysses=pair)

    def order(p):
        m = jnp.minimum(z, U - 1 - z)
        half = (p + 1) // 2
        near_z = jnp.where(lax.rem(p, 2) == 1, z + side * half, z - side * half)
        far_z = jnp.where(z < U - 1 - z, p, U - 1 - p)
        return jnp.where(p <= 2 * m, near_z, far_z)

    def remote(src, dst, send, recv, **where):
        return pltpu.make_async_remote_copy(
            src_ref=src, dst_ref=dst, send_sem=send, recv_sem=recv, device_id=where
        )

    def piece_of(i):
        zz = order(i // SUB)
        return zz, zz * SUB + lax.rem(i, SUB)

    def z_copy(slot, send, target):
        return remote(g.at[slot, t], g.at[slot, t], send, zr.at[slot], ulysses=target)

    def x_copy(slot, col, i):
        return remote(g.at[slot, col], g.at[slot, col], xs.at[i], xr.at[i], tensor=far)

    def c_copy(slot, col, i):
        return remote(g.at[slot, col], g.at[slot, col], cs.at[i], cr.at[i], tensor=near)

    def f_copy(slot, col, i):
        return remote(g.at[slot, col], g.at[slot, col], fs.at[i], fr.at[i], tensor=near)

    def kv_copy(who, slot, i, d):
        view = kv.at[who, :, :, pl.ds(pl.multiple_of(slot * R, R), R), :]
        return remote(view, view, ks.at[d - 1, i], kr.at[who, i], blk=lax.rem(y + d, B))

    def forward(i, act):
        zz, slot = piece_of(i)
        own = i < SUB
        s = lax.rem(i, SUB)

        @pl.when(own & (z + 1 < U))
        def _():
            act(z_copy(slot, up_s.at[s], z + 1))

        @pl.when(own & (z > 0))
        def _():
            act(z_copy(slot, dn_s.at[s], z - 1))

        nxt = jnp.where(zz < z, z + 1, z - 1)

        @pl.when(jnp.logical_not(own) & (nxt >= 0) & (nxt < U))
        def _():
            act(z_copy(slot, zs.at[slot], nxt))

    def step(j, carry):
        @pl.when(j < N)
        def _():
            zz, slot = piece_of(j)

            @pl.when(j >= SUB)
            def _():
                z_copy(slot, zs.at[slot], lax.rem(z + 1, U)).wait_recv()

            forward(j, lambda c: c.start())

            @pl.when(jnp.logical_not(skipped(j)))
            def _():
                x_copy(slot, t, j).start()

            c_copy(slot, t, j).start()

        @pl.when(j == N - 1)
        def _():
            for k in range(skips):
                pair_copy(z, k).start()

        @pl.when(j >= LAG)
        def _():
            i = landing(j - LAG)
            zz, slot = piece_of(i)

            @pl.when(jnp.logical_not(skipped(i)))
            def _():
                x_copy(slot, far, i).wait_recv()

            for k in range(skips):
                @pl.when(i == skip_from + k)
                def _():
                    pair_copy(pair, k).wait_recv()

            f_copy(slot, far, i).start()
            c_copy(slot, near, i).wait_recv()

            @pl.when(i == 0)
            def _():
                w_copy.wait()

            f_copy(slot, cross, i).wait_recv()
            for c in range(3):
                acc = jnp.zeros((R, H * HD), F32)
                for k in range(T):
                    acc += jnp.dot(
                        g[slot, k], w[c, pl.ds(k * feats, feats), :], preferred_element_type=F32
                    )
                for h in range(H):
                    val = (acc[:, h * HD:(h + 1) * HD] * scale_ref[c, h]).astype(BF16)
                    at = pl.ds(pl.multiple_of(slot * R, R), R)
                    if c == 0:
                        q[h, at, :] = val
                    else:
                        kv[y, c - 1, h, at, :] = val
            for d in range(1, B):
                kv_copy(y, slot, i, d).start()

        return carry

    lax.fori_loop(0, N + LAG, step, 0)

    def kv_wait(i, carry):
        zz, slot = piece_of(i)
        for d in range(1, B):
            kv_copy(lax.rem(y + d, B), slot, i, d).wait_recv()
        return carry

    lax.fori_loop(0, N, kv_wait, 0)

    log2e = 1.4426950408889634
    factor = log2e / math.sqrt(HD)

    def a_copy(zz, src):
        return remote(att.at[zz], arr.at[src], as_.at[zz], ar.at[src], ulysses=zz)

    def attend(p, carry):
        zz = order(U - 1 - p)
        for h in range(H):
            qv = q[h, pl.ds(pl.multiple_of(zz * rows, rows), rows), :]

            def keys(b, state):
                high, den, num = state
                s = lax.dot_general(
                    qv, kv[b, 0, h], (((1,), (1,)), ((), ())), preferred_element_type=F32
                )
                lines = []
                for r in range(nbp):
                    qb = (zz * B + y) * nbp + r
                    lines.append(
                        jnp.concatenate(
                            [
                                bias_ref[h, qb, pl.ds((k // nbp * B + b) * nbp + k % nbp, 1), :]
                                for k in range(U * nbp)
                            ],
                            axis=1,
                        )
                    )
                s = jnp.concatenate(
                    [s[r * block:(r + 1) * block] * factor + lines[r] for r in range(nbp)], axis=0
                )
                new = jnp.maximum(high, jnp.max(s, axis=1, keepdims=True))
                wts = jnp.exp2(s - new)
                fix = jnp.exp2(high - new)
                den = den * fix + jnp.sum(wts, axis=1, keepdims=True)
                num = num * fix + jnp.dot(
                    wts.astype(BF16), kv[b, 1, h], preferred_element_type=F32
                )
                return new, den, num

            start = (
                jnp.full((rows, 1), -1e30, F32),
                jnp.zeros((rows, 1), F32),
                jnp.zeros((rows, HD), F32),
            )
            high, den, num = lax.fori_loop(0, B, keys, start)
            att[zz, :, h * HD:(h + 1) * HD] = (num / den).astype(BF16)

        @pl.when(p < U - 1)
        def _():
            a_copy(zz, z).start()

        return carry

    lax.fori_loop(0, U, attend, 0)
    arr[z] = att[z]
    for c in wo_copies:
        c.wait()
    for d in range(1, U):
        a_copy(lax.rem(z + d, U), lax.rem(z + d, U)).wait_recv()

    def product(col):
        acc = jnp.dot(arr[0], wo[col, 0], preferred_element_type=F32)
        for u in range(1, U):
            acc += jnp.dot(arr[u], wo[col, u], preferred_element_type=F32)
        return acc

    def p_copy(k):
        return remote(part.at[k], got.at[k], ps.at[k], pr.at[k], tensor=near)

    m_copy = remote(mid, far_got, ms, mr, tensor=far)
    part[0] = product(cross).astype(BF16)
    p_copy(0).start()
    there = product(far)
    p_copy(0).wait_recv()
    mid[...] = (there + got[0].astype(F32)).astype(BF16)
    m_copy.start()
    part[1] = product(near).astype(BF16)
    p_copy(1).start()
    here = product(t)
    p_copy(1).wait_recv()
    here = here + got[1].astype(F32)
    m_copy.wait_recv()
    out_ref[...] = (here + far_got[...].astype(F32)).astype(BF16)

    def drain(i, carry):
        zz, slot = piece_of(i)
        forward(i, lambda c: c.wait_send())

        @pl.when(jnp.logical_not(skipped(i)))
        def _():
            x_copy(slot, t, i).wait_send()

        c_copy(slot, t, i).wait_send()
        f_copy(slot, far, i).wait_send()
        for d in range(1, B):
            kv_copy(y, slot, i, d).wait_send()
        return carry

    lax.fori_loop(0, N, drain, 0)
    for k in range(skips):
        pair_copy(z, k).wait_send()
    for d in range(1, U):
        a_copy(lax.rem(z + d, U), z).wait_send()
    p_copy(0).wait_send()
    p_copy(1).wait_send()
    m_copy.wait_send()


def local(tokens, w_qkv, qkv_scale, block_mask, w_out):
    U, B, T = lax.axis_size("ulysses"), lax.axis_size("blk"), lax.axis_size("tensor")
    rows, feats = tokens.shape
    heads, blocks = block_mask.shape[0], block_mask.shape[1]
    cols = w_qkv.shape[2]
    hd = cols // heads
    block = U * B * rows // blocks
    ids = jnp.arange(blocks)
    allowed = (block_mask == 1) | (ids[:, None] == ids[None, :])[None]
    bias = jnp.broadcast_to(
        jnp.where(allowed, 0.0, -jnp.inf).astype(F32)[..., None], (heads, blocks, blocks, block)
    )
    R, N = rows // SUB, U * SUB
    dma = lambda *s: pltpu.SemaphoreType.DMA(s)
    vmem = pl.BlockSpec(memory_space=pltpu.VMEM)
    hbm = pl.BlockSpec(memory_space=pl.ANY)
    return pl.pallas_call(
        functools.partial(kernel, U, B, T),
        out_shape=jax.ShapeDtypeStruct((rows, feats), BF16),
        in_specs=[vmem, hbm, pl.BlockSpec(memory_space=pltpu.SMEM), vmem, hbm],
        out_specs=vmem,
        scratch_shapes=[
            pltpu.VMEM((N, T, R, feats), BF16),
            pltpu.VMEM((3, T * feats, cols), BF16),
            pltpu.VMEM((T, U, cols, feats), BF16),
            pltpu.VMEM((heads, U * rows, hd), BF16),
            pltpu.VMEM((B, 2, heads, U * rows, hd), BF16),
            pltpu.VMEM((U, rows, cols), BF16),
            pltpu.VMEM((U, rows, cols), BF16),
            pltpu.VMEM((2, rows, feats), BF16),
            pltpu.VMEM((2, rows, feats), BF16),
            pltpu.VMEM((rows, feats), BF16),
            pltpu.VMEM((rows, feats), BF16),
            pltpu.SemaphoreType.DMA,
            dma(T),
            dma(SUB),
            dma(N), dma(N), dma(SUB), dma(SUB),
            dma(N), dma(N), dma(N), dma(N), dma(N), dma(N),
            dma(B, N), dma(B, N),
            dma(U), dma(U),
            dma(2), dma(2),
            pltpu.SemaphoreType.DMA, pltpu.SemaphoreType.DMA,
            dma(SUB), dma(SUB),
        ],
        compiler_params=pltpu.CompilerParams(
            collective_id=0, has_side_effects=True, vmem_limit_bytes=62 * 1024 * 1024
        ),
    )(tokens, jnp.transpose(w_qkv, (1, 0, 2)), qkv_scale, bias, w_out)


def solution(mesh):
    return jax.shard_map(
        local,
        mesh=mesh,
        in_specs=(
            P(("ulysses", "blk"), "tensor"),
            P(None, None, ("ulysses", "tensor")),
            P(None, ("ulysses", "tensor")),
            P(("ulysses", "tensor"), None, None),
            P(None, "tensor", None),
        ),
        out_specs=P(("ulysses", "blk"), "tensor"),
        check_vma=False,
    )
```

```python
import functools
import math

import jax
import jax.numpy as jnp
from jax import lax
from jax.experimental import pallas as pl
from jax.experimental.pallas import tpu as pltpu
from jax.sharding import PartitionSpec as P

SUB = 2
LAG = 2 * SUB
HALVES = 2
F32 = jnp.float32
BF16 = jnp.bfloat16


def kernel(U, B, T, x_ref, w_hbm, scale_ref, bias_ref, wo_hbm, out_ref,
           g, w, wo, q, kv, att, arr, part, got, mid, far_got,
           w_sem, wo_sem, own_sem,
           zs, zr, up_s, dn_s, xs, xr, cs, cr, fs, fr, ks, kr, as_, ar, ps, pr, ms, mr, hs, hr):
    z, y, t = lax.axis_index("ulysses"), lax.axis_index("blk"), lax.axis_index("tensor")
    near = t + 1 - 2 * lax.rem(t, 2)
    far = lax.rem(t + T // 2, T)
    cross = lax.rem(near + T // 2, T)
    rows, feats = x_ref.shape
    R = rows // SUB
    H, HD = q.shape[0], q.shape[2]
    N = U * SUB
    nbp = rows // bias_ref.shape[3]
    block = bias_ref.shape[3]

    def own_copy(s):
        return pltpu.make_async_copy(x_ref.at[pl.ds(s * R, R)], g.at[z * SUB + s, t], own_sem.at[s])

    for s in range(SUB):
        own_copy(s).start()
    w_copy = pltpu.make_async_copy(w_hbm, w, w_sem)
    wo_copies = [
        pltpu.make_async_copy(wo_hbm.at[:, :, pl.ds(j * feats, feats)], wo.at[j], wo_sem.at[j])
        for j in range(T)
    ]

    barrier = pltpu.get_barrier_semaphore()
    for d in range(1, U):
        pl.semaphore_signal(barrier, inc=1, device_id={"ulysses": lax.rem(z + d, U)})
    for d in range(1, B):
        pl.semaphore_signal(barrier, inc=1, device_id={"blk": lax.rem(y + d, B)})
    pl.semaphore_signal(barrier, inc=1, device_id={"tensor": near})
    pl.semaphore_signal(barrier, inc=1, device_id={"tensor": far})
    pl.semaphore_wait(barrier, (U - 1) + (B - 1) + 2)

    side = 1 - 2 * lax.rem(z, 2)
    pair = z + side
    skip_from = SUB + SUB // 2
    skips = 2 * SUB - skip_from

    def skipped(j):
        return (j >= skip_from) & (j < skip_from + skips)

    def landing(i):
        late = jnp.where(i < N - skips, i + skips, i - (N - skips) + skip_from)
        return jnp.where(i < skip_from, i, late)

    def pair_copy(owner, j):
        slot = owner * SUB + SUB // 2 + j
        view = g.at[slot, far]
        return remote(view, view, hs.at[j], hr.at[j], ulysses=pair)

    for s in range(SUB):
        own_copy(s).wait()

    def order(p):
        m = jnp.minimum(z, U - 1 - z)
        half = (p + 1) // 2
        near_z = jnp.where(lax.rem(p, 2) == 1, z + side * half, z - side * half)
        far_z = jnp.where(z < U - 1 - z, p, U - 1 - p)
        return jnp.where(p <= 2 * m, near_z, far_z)

    def remote(src, dst, send, recv, **where):
        return pltpu.make_async_remote_copy(
            src_ref=src, dst_ref=dst, send_sem=send, recv_sem=recv, device_id=where
        )

    def piece_of(i):
        zz = order(i // SUB)
        return zz, zz * SUB + lax.rem(i, SUB)

    def z_copy(slot, send, target):
        return remote(g.at[slot, t], g.at[slot, t], send, zr.at[slot], ulysses=target)

    def x_copy(slot, col, i):
        return remote(g.at[slot, col], g.at[slot, col], xs.at[i], xr.at[i], tensor=far)

    def c_copy(slot, col, i):
        return remote(g.at[slot, col], g.at[slot, col], cs.at[i], cr.at[i], tensor=near)

    def f_copy(slot, col, i):
        return remote(g.at[slot, col], g.at[slot, col], fs.at[i], fr.at[i], tensor=near)

    def kv_copy(who, slot, i, d):
        view = kv.at[who, :, :, pl.ds(pl.multiple_of(slot * R, R), R), :]
        return remote(view, view, ks.at[d - 1, i], kr.at[who, i], blk=lax.rem(y + d, B))

    def forward(i, act):
        zz, slot = piece_of(i)
        own = i < SUB
        s = lax.rem(i, SUB)

        @pl.when(own & (z + 1 < U))
        def _():
            act(z_copy(slot, up_s.at[s], z + 1))

        @pl.when(own & (z > 0))
        def _():
            act(z_copy(slot, dn_s.at[s], z - 1))

        nxt = jnp.where(zz < z, z + 1, z - 1)

        @pl.when(jnp.logical_not(own) & (nxt >= 0) & (nxt < U))
        def _():
            act(z_copy(slot, zs.at[slot], nxt))

    def step(j, carry):
        @pl.when(j < N)
        def _():
            zz, slot = piece_of(j)

            @pl.when(j >= SUB)
            def _():
                z_copy(slot, zs.at[slot], lax.rem(z + 1, U)).wait_recv()

            forward(j, lambda c: c.start())

            @pl.when(jnp.logical_not(skipped(j)))
            def _():
                x_copy(slot, t, j).start()

            c_copy(slot, t, j).start()

        @pl.when(j == SUB - 1)
        def _():
            w_copy.start()

        @pl.when(j == 2 * SUB)
        def _():
            for c in wo_copies:
                c.start()

        @pl.when(j == N - 1)
        def _():
            for k in range(skips):
                pair_copy(z, k).start()

        @pl.when(j >= LAG)
        def _():
            i = landing(j - LAG)
            zz, slot = piece_of(i)

            @pl.when(jnp.logical_not(skipped(i)))
            def _():
                x_copy(slot, far, i).wait_recv()

            for k in range(skips):
                @pl.when(i == skip_from + k)
                def _():
                    pair_copy(pair, k).wait_recv()

            f_copy(slot, far, i).start()
            c_copy(slot, near, i).wait_recv()

            @pl.when(i == 0)
            def _():
                w_copy.wait()

            f_copy(slot, cross, i).wait_recv()
            for c in range(3):
                acc = jnp.zeros((R, H * HD), F32)
                for k in range(T):
                    acc += jnp.dot(
                        g[slot, k], w[c, pl.ds(k * feats, feats), :], preferred_element_type=F32
                    )
                for h in range(H):
                    val = (acc[:, h * HD:(h + 1) * HD] * scale_ref[c, h]).astype(BF16)
                    at = pl.ds(pl.multiple_of(slot * R, R), R)
                    if c == 0:
                        q[h, at, :] = val
                    else:
                        kv[y, c - 1, h, at, :] = val
            for d in range(1, B):
                kv_copy(y, slot, i, d).start()

        return carry

    lax.fori_loop(0, N + LAG, step, 0)

    def kv_wait(i, carry):
        zz, slot = piece_of(i)
        for d in range(1, B):
            kv_copy(lax.rem(y + d, B), slot, i, d).wait_recv()
        return carry

    lax.fori_loop(0, N, kv_wait, 0)

    log2e = 1.4426950408889634
    factor = log2e / math.sqrt(HD)

    HR = rows // HALVES
    nbh = nbp // HALVES

    def a_copy(hf, zz, src):
        return remote(
            att.at[hf, zz], arr.at[hf, src], as_.at[hf, zz], ar.at[hf, src], ulysses=zz
        )

    def attend(turn, carry):
        hf, p = turn // U, lax.rem(turn, U)
        zz = order(U - 1 - p)
        for h in range(H):
            qv = q[h, pl.ds(pl.multiple_of(zz * rows + hf * HR, HR), HR), :]

            def keys(b, state):
                high, den, num = state
                s = lax.dot_general(
                    qv, kv[b, 0, h], (((1,), (1,)), ((), ())), preferred_element_type=F32
                )
                lines = []
                for r in range(nbh):
                    qb = (zz * B + y) * nbp + hf * nbh + r
                    lines.append(
                        jnp.concatenate(
                            [
                                bias_ref[h, qb, pl.ds((k // nbp * B + b) * nbp + k % nbp, 1), :]
                                for k in range(U * nbp)
                            ],
                            axis=1,
                        )
                    )
                s = jnp.concatenate(
                    [s[r * block:(r + 1) * block] * factor + lines[r] for r in range(nbh)], axis=0
                )
                new = jnp.maximum(high, jnp.max(s, axis=1, keepdims=True))
                wts = jnp.exp2(s - new)
                fix = jnp.exp2(high - new)
                den = den * fix + jnp.sum(wts, axis=1, keepdims=True)
                num = num * fix + jnp.dot(
                    wts.astype(BF16), kv[b, 1, h], preferred_element_type=F32
                )
                return new, den, num

            start = (
                jnp.full((HR, 1), -1e30, F32),
                jnp.zeros((HR, 1), F32),
                jnp.zeros((HR, HD), F32),
            )
            high, den, num = lax.fori_loop(0, B, keys, start)
            att[hf, zz, :, h * HD:(h + 1) * HD] = (num / den).astype(BF16)

        @pl.when(p < U - 1)
        def _():
            a_copy(hf, zz, z).start()

        return carry

    lax.fori_loop(0, U * HALVES, attend, 0)
    for c in wo_copies:
        c.wait()

    def product(hf, col):
        acc = jnp.dot(arr[hf, 0], wo[col, 0], preferred_element_type=F32)
        for u in range(1, U):
            acc += jnp.dot(arr[hf, u], wo[col, u], preferred_element_type=F32)
        return acc

    def p_copy(hf, k):
        return remote(part.at[hf, k], got.at[hf, k], ps.at[hf, k], pr.at[hf, k], tensor=near)

    def m_copy(hf):
        return remote(mid.at[hf], far_got.at[hf], ms.at[hf], mr.at[hf], tensor=far)

    for hf in range(HALVES):
        arr[hf, z] = att[hf, z]
        for d in range(1, U):
            a_copy(hf, lax.rem(z + d, U), lax.rem(z + d, U)).wait_recv()
        part[hf, 0] = product(hf, cross).astype(BF16)
        p_copy(hf, 0).start()
        there = product(hf, far)
        p_copy(hf, 0).wait_recv()
        mid[hf] = (there + got[hf, 0].astype(F32)).astype(BF16)
        m_copy(hf).start()
        part[hf, 1] = product(hf, near).astype(BF16)
        p_copy(hf, 1).start()
    for hf in range(HALVES):
        here = product(hf, t)
        p_copy(hf, 1).wait_recv()
        here = here + got[hf, 1].astype(F32)
        m_copy(hf).wait_recv()
        out_ref[hf * HR:(hf + 1) * HR, :] = (here + far_got[hf].astype(F32)).astype(BF16)

    def drain(i, carry):
        zz, slot = piece_of(i)
        forward(i, lambda c: c.wait_send())

        @pl.when(jnp.logical_not(skipped(i)))
        def _():
            x_copy(slot, t, i).wait_send()

        c_copy(slot, t, i).wait_send()
        f_copy(slot, far, i).wait_send()
        for d in range(1, B):
            kv_copy(y, slot, i, d).wait_send()
        return carry

    lax.fori_loop(0, N, drain, 0)
    for k in range(skips):
        pair_copy(z, k).wait_send()
    for hf in range(HALVES):
        for d in range(1, U):
            a_copy(hf, lax.rem(z + d, U), z).wait_send()
        p_copy(hf, 0).wait_send()
        p_copy(hf, 1).wait_send()
        m_copy(hf).wait_send()


def local(tokens, w_qkv, qkv_scale, block_mask, w_out):
    U, B, T = lax.axis_size("ulysses"), lax.axis_size("blk"), lax.axis_size("tensor")
    rows, feats = tokens.shape
    heads, blocks = block_mask.shape[0], block_mask.shape[1]
    cols = w_qkv.shape[2]
    hd = cols // heads
    block = U * B * rows // blocks
    ids = jnp.arange(blocks)
    allowed = (block_mask == 1) | (ids[:, None] == ids[None, :])[None]
    bias = jnp.broadcast_to(
        jnp.where(allowed, 0.0, -jnp.inf).astype(F32)[..., None], (heads, blocks, blocks, block)
    )
    R, N = rows // SUB, U * SUB
    dma = lambda *s: pltpu.SemaphoreType.DMA(s)
    vmem = pl.BlockSpec(memory_space=pltpu.VMEM)
    hbm = pl.BlockSpec(memory_space=pl.ANY)
    return pl.pallas_call(
        functools.partial(kernel, U, B, T),
        out_shape=jax.ShapeDtypeStruct((rows, feats), BF16),
        in_specs=[vmem, hbm, pl.BlockSpec(memory_space=pltpu.SMEM), vmem, hbm],
        out_specs=vmem,
        scratch_shapes=[
            pltpu.VMEM((N, T, R, feats), BF16),
            pltpu.VMEM((3, T * feats, cols), BF16),
            pltpu.VMEM((T, U, cols, feats), BF16),
            pltpu.VMEM((heads, U * rows, hd), BF16),
            pltpu.VMEM((B, 2, heads, U * rows, hd), BF16),
            pltpu.VMEM((HALVES, U, rows // HALVES, cols), BF16),
            pltpu.VMEM((HALVES, U, rows // HALVES, cols), BF16),
            pltpu.VMEM((HALVES, 2, rows // HALVES, feats), BF16),
            pltpu.VMEM((HALVES, 2, rows // HALVES, feats), BF16),
            pltpu.VMEM((HALVES, rows // HALVES, feats), BF16),
            pltpu.VMEM((HALVES, rows // HALVES, feats), BF16),
            pltpu.SemaphoreType.DMA,
            dma(T),
            dma(SUB),
            dma(N), dma(N), dma(SUB), dma(SUB),
            dma(N), dma(N), dma(N), dma(N), dma(N), dma(N),
            dma(B, N), dma(B, N),
            dma(HALVES, U), dma(HALVES, U),
            dma(HALVES, 2), dma(HALVES, 2),
            dma(HALVES), dma(HALVES),
            dma(SUB), dma(SUB),
        ],
        compiler_params=pltpu.CompilerParams(
            collective_id=0, has_side_effects=True, vmem_limit_bytes=62 * 1024 * 1024
        ),
    )(tokens, jnp.transpose(w_qkv, (1, 0, 2)), qkv_scale, bias, w_out)


def solution(mesh):
    return jax.shard_map(
        local,
        mesh=mesh,
        in_specs=(
            P(("ulysses", "blk"), "tensor"),
            P(None, None, ("ulysses", "tensor")),
            P(None, ("ulysses", "tensor")),
            P(("ulysses", "tensor"), None, None),
            P(None, "tensor", None),
        ),
        out_specs=P(("ulysses", "blk"), "tensor"),
        check_vma=False,
    )
```
